512 devices in a mesh: rep: 8 (over y, core), exp: 64 (over x, z).
Axes of the slice: x: 4, y: 4, z: 16, core: 2. Of those that a mesh axis runs over, the one named last changes fastest.
Arguments:
- payload: bfloat16 [16384, 2048], P(('rep', 'exp')), may hold values from -6 to 6
- block_scales: bfloat16 [16384, 16], P(('rep', 'exp')), may hold values from 0.29882812 to 3
- cotangent: bfloat16 [16384, 2048], P(('rep', 'exp')), may hold values from -12 to 12
- expert_ids: int32 [16384, 8], P(('rep', 'exp')), may hold values from 0 to 63, all different within a row; in each aligned block of 32 rows (0 to 31, 32 to 63, ...) at most 5 rows name the same one
- route_counts: int32 [16384, 8], P(('rep', 'exp')), may hold values from 1 to 15
- gate_up: bfloat16 [64, 2, 2048, 384], P('exp', None, 'rep'), may hold values from -0.125 to 0.125
- down_weight: bfloat16 [64, 384, 2048], P('exp', None, 'rep'), may hold values from -0.3125 to 0.3125
- first_moment: float32 [64, 2, 2048, 384], P('exp', None, 'rep'), may hold values from -12 to 12
- second_moment: float32 [64, 2, 2048, 384], P('exp', None, 'rep'), may hold values from 10 to 300
Outputs:
- d_activation: bfloat16 [16384, 2048], P(('rep', 'exp'))
- new_first: float32 [64, 2, 2048, 384], P('exp', None, 'rep')
- new_second: float32 [64, 2, 2048, 384], P('exp', None, 'rep')
- weight_step: bfloat16 [64, 2, 2048, 384], P('exp', None, 'rep')
The draws below stay inside these ranges and needn't reach their ends.
Inputs may be any that keep to these rules, and one draw needn't show every extreme that they name: `expert_ids`: in the rows of one device (aligned blocks of 32 tokens) no expert is named more than 5 times, a bound that some block reaches; each token names 8 different experts.
All inputs are finite; a program needn't handle non-finite values.
Results may differ from the reference program's by a relative error of at most 0.02.
Values may be sent and summed in bfloat16 or wider, within the bound.
A program may use at most 64 MiB of HBM per device.

```python
import math
import jax
import jax.numpy as jnp
import numpy as np
from jax import lax

D = 2048
FF = 384
TOP = 8
QB = 128
TOK_DEV = 32
EXPERTS = 64
TOKENS = 16384
CAP = 5
N_REP = 8
N_EXP = 64


def draw_cotangent(key, part):
    rows = jnp.arange(TOKENS, dtype=jnp.float32)[:, None]
    ramp = jnp.exp(jnp.log(3.0) * rows / TOKENS)
    base = jnp.clip(jax.random.normal(key, (TOKENS, D), jnp.float32), -4.0, 4.0)
    return (base * ramp).astype(jnp.bfloat16)


def with_ends(values, stream_key, smallest, largest):
    place = [jax.random.randint(jax.random.fold_in(stream_key, axis), (), 0, length) for axis, length in enumerate(values.shape)]
    widest = values.shape.index(max(values.shape))
    beside = place[:widest] + [(place[widest] + 1) % values.shape[widest]] + place[widest + 1:]
    return values.at[tuple(place)].set(smallest).at[tuple(beside)].set(largest)


def shard_levels(stream_key, shape, cuts, least, largest):
    def one(dim, blocks):
        draws = jax.random.uniform(jax.random.fold_in(jax.random.fold_in(stream_key, 6), dim), (blocks,), jnp.float32, least / len(cuts), largest / len(cuts))
        return jnp.repeat(jnp.exp(draws), shape[dim] // blocks).reshape((-1,) + (1,) * (len(shape) - dim - 1))

    gain = one(*cuts[0])
    for cut in cuts[1:]:
        gain = gain * one(*cut)
    return gain


def shared_out(key, own, number, rows, number_of, top, reach, lean):
    sequence = jax.random.permutation(key, number_of)
    crowded, ordinary = load_shares(number_of, rows * top, reach, lean, True), load_shares(number_of, rows * top, reach, lean, False)
    places = jnp.arange(number_of)

    def named(sizes, offset_by):
        used = int((sizes > 0).sum())
        fixed = max(1, used // 4)
        passed = fixed + (places - fixed + offset_by * (used - fixed)) % max(1, number_of - fixed)
        return jnp.zeros((number_of,), jnp.int32).at[sequence[jnp.where(places < fixed, places, passed)]].set(jnp.asarray(sizes, jnp.int32))

    sizes = jnp.where(number % 4 == 0, named(crowded, number // 4), named(ordinary, number - number // 4 - 1))
    mixed = jax.random.permutation(jax.random.fold_in(own, 3), number_of)
    source_of, receiver = mixed[0:number_of // 2 * 2:2], mixed[1:number_of // 2 * 2:2]
    slack = jnp.minimum(sizes[source_of] - 1, reach - sizes[receiver]) // 2
    slack = jnp.where((source_of == sequence[0]) | (receiver == sequence[0]) | (sizes[receiver] == 0), 0, jnp.maximum(slack, 0))
    passed = jax.random.randint(jax.random.fold_in(own, 4), (number_of // 2,), 0, 1 << 20) % (slack + 1)
    sizes = sizes.at[source_of].add(-passed).at[receiver].add(passed)
    labels = jnp.searchsorted(jnp.cumsum(sizes), jnp.arange(rows * top), side="right").astype(jnp.int32)
    table = labels.reshape(top, rows).T
    table = table[jax.random.permutation(jax.random.fold_in(own, 1), rows)]
    offset_by = jax.random.randint(jax.random.fold_in(own, 2), (rows, 1), 0, top)
    return jnp.take_along_axis(table, (jnp.arange(top)[None, :] + offset_by) % top, axis=1)


def load_shares(count, total, reach, skew, full):
    portions = [(1 << 20) // math.isqrt(standing ** skew) + 1 for standing in range(1, count + 1)]
    largest = reach if full else min(reach, max(-(-total // count), total * portions[0] // sum(portions)))
    least = 1 if total - largest >= count - 1 else 0
    given, rest = [largest] + [least] * (count - 1), total - largest - least * (count - 1)
    while rest > 0:
        candidates = [i for i in range(1, count) if given[i] < largest] or [i for i in range(1, count) if given[i] < reach]
        whole, left = sum([portions[i] for i in candidates]), rest
        for i in candidates:
            more = min(reach - given[i], max(1, left * portions[i] // whole), rest)
            given[i] = given[i] + more
            rest = rest - more
    return np.array(given)


def gaussian(own_key, dims, spread, most, cuts=(), kind=jnp.bfloat16):
    level = shard_levels(own_key, dims, cuts, -0.22, 0.18) if cuts else 1.0
    drawn = jax.random.normal(own_key, dims, jnp.float32) * spread * level
    return jnp.minimum(jnp.maximum(drawn, -most), most).astype(kind)


def setup_inputs(seed: int = 0) -> dict:
    keys = jax.random.split(jax.random.key(seed), 10)
    payload = gaussian(keys[0], (TOKENS, D), 1.0, 6.0, ((0, 512),))
    block_scales = jnp.clip(jnp.exp(math.log(3.0) - 2.306499 * jax.random.uniform(keys[1], (TOKENS, D // QB), jnp.float32) ** shard_levels(keys[1], (TOKENS, D // QB), ((0, 512),), -0.2, 0.2)), 0.29882812, 3.0).astype(jnp.bfloat16)
    cotangent = draw_cotangent(jax.random.fold_in(keys[9], 71), 0)
    expert_ids_keys = jax.random.split(jax.random.fold_in(keys[3], 1), TOKENS // TOK_DEV)
    expert_ids_turns = jax.random.permutation(jax.random.fold_in(keys[3], 3), TOKENS // TOK_DEV)
    expert_ids = jax.vmap(lambda own, number: shared_out(jax.random.fold_in(keys[3], 2), own, number, TOK_DEV, EXPERTS, TOP, CAP, 2))(expert_ids_keys, expert_ids_turns).reshape((TOKENS, TOP))
    route_counts = with_ends(jax.random.randint(keys[4], (TOKENS, TOP), 1, 16), jax.random.fold_in(keys[4], 1), 1, 15).astype(jnp.int32)
    gate_up = gaussian(keys[5], (EXPERTS, 2, D, FF), D ** -0.5, 0.125, ((0, 64), (2, 8)))
    down_weight = gaussian(keys[6], (EXPERTS, FF, D), FF ** -0.5, 0.3125, ((0, 64), (2, 8)))
    first_moment = gaussian(keys[7], (EXPERTS, 2, D, FF), 3.0, 12.0, ((0, 64), (2, 8)), jnp.float32)
    second_moment = jnp.clip(jnp.exp(math.log(300.0) - 3.4011974 * jax.random.uniform(keys[8], (EXPERTS, 2, D, FF), jnp.float32) ** shard_levels(keys[8], (EXPERTS, 2, D, FF), ((0, 64), (2, 8)), -0.2, 0.2)), 10.0, 300.0)
    return {"payload": payload, "block_scales": block_scales, "cotangent": cotangent, "expert_ids": expert_ids, "route_counts": route_counts, "gate_up": gate_up, "down_weight": down_weight, "first_moment": first_moment, "second_moment": second_moment}


def silu_parts(gate_pre):
    sigmoid_val = jax.nn.sigmoid(gate_pre)
    return (gate_pre * sigmoid_val, sigmoid_val * (1.0 + gate_pre * (1.0 - sigmoid_val)))

def reference(payload, block_scales, cotangent, expert_ids, route_counts, gate_up, down_weight, first_moment, second_moment):
    slot_count = N_EXP * CAP
    pair_count = TOK_DEV * TOP
    device_total = N_REP * N_EXP
    all_pairs = device_total * pair_count
    count_float = route_counts.astype(jnp.float32)
    route_share = count_float / lax.optimization_barrier(jnp.sum(count_float, axis=1, keepdims=True))
    device_ids = expert_ids.reshape(device_total, pair_count)
    onehot = (device_ids[:, :, None] == jnp.arange(EXPERTS, dtype=jnp.int32)[None, None, :]).astype(jnp.int32)
    slot_rank = lax.optimization_barrier(jnp.sum((jnp.cumsum(onehot, axis=1) - 1) * onehot, axis=2))
    device_index = jnp.arange(device_total, dtype=jnp.int32)[:, None]
    replica_of = jnp.broadcast_to(device_index // N_EXP, device_ids.shape)
    position = device_index % N_EXP * CAP + slot_rank
    flat_pair = device_index * pair_count + jnp.arange(pair_count, dtype=jnp.int32)[None, :]
    slot_table = jnp.full((N_REP, EXPERTS, slot_count), all_pairs, jnp.int32)
    slot_table = slot_table.at[replica_of, device_ids, position].set(flat_pair)
    entry_count = 2.0 * D * FF

    def expert_step(accumulated, inputs):
        expert_table, weights_gu, weights_down, moment_one, moment_two = inputs
        filled = (expert_table < all_pairs)[:, :, None]
        pair_index = jnp.minimum(expert_table, all_pairs - 1)
        token_index = pair_index // TOP
        route_slot = pair_index % TOP
        blocked = payload[token_index].astype(jnp.float32).reshape(N_REP, slot_count, D // QB, QB)
        scaled = blocked * block_scales[token_index].astype(jnp.float32)[..., None]
        input_rows = jnp.where(filled, scaled.reshape(N_REP, slot_count, D), 0.0).astype(jnp.bfloat16)
        share_rows = route_share[token_index, route_slot][:, :, None]
        cotan_rows = jnp.where(filled, share_rows * cotangent[token_index].astype(jnp.float32), 0.0).astype(jnp.bfloat16)
        flat_inputs = input_rows.reshape(N_REP * slot_count, D)
        gate_pre = jnp.dot(flat_inputs, weights_gu[0], preferred_element_type=jnp.float32)
        up_pre = jnp.dot(flat_inputs, weights_gu[1], preferred_element_type=jnp.float32)
        hidden_grad = jnp.dot(cotan_rows.reshape(N_REP * slot_count, D), weights_down.T, preferred_element_type=jnp.float32)
        silu_val, silu_slope = silu_parts(gate_pre)
        gate_grad = (hidden_grad * up_pre * silu_slope).astype(jnp.bfloat16)
        up_grad = (hidden_grad * silu_val).astype(jnp.bfloat16)
        row_grad = (jnp.dot(gate_grad, weights_gu[0].T, preferred_element_type=jnp.float32) + jnp.dot(up_grad, weights_gu[1].T, preferred_element_type=jnp.float32)).astype(jnp.bfloat16)
        added = jnp.where(filled.reshape(N_REP * slot_count, 1), row_grad.astype(jnp.float32), 0.0)
        accumulated = accumulated.at[token_index.reshape(N_REP * slot_count)].add(added)
        inputs_wide = input_rows.astype(jnp.float32)
        gate_wide = gate_grad.reshape(N_REP, slot_count, FF).astype(jnp.float32)
        up_wide = up_grad.reshape(N_REP, slot_count, FF).astype(jnp.float32)
        replica_grad = jnp.stack([jnp.einsum('rsd,rsf->rdf', inputs_wide, gate_wide), jnp.einsum('rsd,rsf->rdf', inputs_wide, up_wide)], axis=1).astype(jnp.bfloat16)
        replica_exact = lax.optimization_barrier(replica_grad).astype(jnp.float32)
        small_norm = jnp.sum(replica_exact * replica_exact) / (N_REP * entry_count)
        total_grad = lax.optimization_barrier(jnp.sum(replica_exact, axis=0))
        big_norm = jnp.sum(total_grad * total_grad) / (N_REP * N_REP * entry_count)
        noise_gain = N_REP * big_norm / (small_norm + 1e-06)
        new_first = 0.9 * moment_one + 0.1 * total_grad
        new_second = 0.95 * moment_two + 0.05 * total_grad * total_grad
        weight_step = (noise_gain * new_first / (jnp.sqrt(new_second) + 1e-08)).astype(jnp.bfloat16)
        return (accumulated, (new_first, new_second, weight_step))
    grad_start = jnp.zeros((TOKENS, D), jnp.float32)
    accumulated, outputs = lax.scan(expert_step, grad_start, (slot_table.transpose(1, 0, 2), gate_up, down_weight, first_moment, second_moment))
    return (accumulated.astype(jnp.bfloat16), outputs[0], outputs[1], outputs[2])
```

```python
import jax
import jax.numpy as jnp
import numpy as np
from jax import lax
from jax.sharding import PartitionSpec as P

X_SIZE = 4
Z_SIZE = 16
CAPACITY = 5
Z_GROUPS = [[x * Z_SIZE + z for z in range(Z_SIZE)] for x in range(X_SIZE)]
X_GROUPS = [[x * Z_SIZE + z for x in range(X_SIZE)] for z in range(Z_SIZE)]


def silu_parts(gate_pre):
    sigmoid_val = jax.nn.sigmoid(gate_pre)
    return (gate_pre * sigmoid_val, sigmoid_val * (1.0 + gate_pre * (1.0 - sigmoid_val)))


def dequantize(values, scales):
    array_shape = values.shape
    blocked = values.astype(jnp.float32).reshape(
        array_shape[:-1] + (scales.shape[-1], array_shape[-1] // scales.shape[-1])
    )
    return (
        (blocked * scales.astype(jnp.float32)[..., None]).reshape(array_shape).astype(jnp.bfloat16)
    )


def route_tables(ids, counts, z_pos, tok_rows):
    count_float = counts.astype(jnp.float32)
    share = count_float / jnp.sum(count_float, axis=1, keepdims=True)
    experts = jnp.arange(X_SIZE, dtype=jnp.int32) * Z_SIZE + z_pos
    hit = ids[None] == experts[:, None, None]
    match = jnp.any(hit, axis=2)
    weight = jnp.sum(jnp.where(hit, share[None], 0.0), axis=2)
    ones = match.astype(jnp.bfloat16).reshape(X_SIZE * Z_SIZE, tok_rows)
    before = jnp.asarray(np.triu(np.ones((tok_rows, tok_rows)), 1), jnp.bfloat16)
    rank = jnp.dot(ones, before, preferred_element_type=jnp.float32).astype(jnp.int32)
    base = jnp.arange(Z_SIZE, dtype=jnp.int32)[None, :, None] * CAPACITY
    slot = (base + rank.reshape(X_SIZE, Z_SIZE, tok_rows)).reshape(X_SIZE, Z_SIZE * tok_rows)
    slot = jnp.where(match, slot, -1)
    lanes = jnp.arange(Z_SIZE * CAPACITY, dtype=jnp.int32)
    pick = slot[:, None, :] == lanes[None, :, None]
    slot_share = jnp.sum(jnp.where(pick, weight[:, None, :], 0.0), axis=2)
    pick = pick.reshape(X_SIZE * Z_SIZE * CAPACITY, Z_SIZE * tok_rows).astype(jnp.bfloat16)
    return pick, slot_share.reshape(X_SIZE * Z_SIZE * CAPACITY)


def on_device(
    payload,
    block_scales,
    cotangent,
    expert_ids,
    route_counts,
    gate_up,
    down_weight,
    first_moment,
    second_moment,
):
    tok_rows, width = payload.shape
    replicas = lax.axis_size("rep")
    z_pos = lax.axis_index("exp") % Z_SIZE
    side = Z_SIZE * CAPACITY
    slot_count = X_SIZE * side

    activation = dequantize(payload, block_scales)
    routing = jnp.concatenate([expert_ids, route_counts], axis=1).astype(jnp.bfloat16)
    routing = jnp.pad(routing, ((0, 0), (0, 112)))
    act_all = lax.all_gather(
        jnp.concatenate([activation, routing], axis=1),
        "exp",
        axis=0,
        tiled=True,
        axis_index_groups=Z_GROUPS,
    )
    cot_all = lax.all_gather(cotangent, "exp", axis=0, tiled=True, axis_index_groups=Z_GROUPS)
    whole_gate_up = lax.all_gather(gate_up, "rep", axis=2, tiled=True)
    whole_down = lax.all_gather(down_weight, "rep", axis=2, tiled=True)

    top = expert_ids.shape[1]
    ids = act_all[:, width : width + top].astype(jnp.int32)
    counts = act_all[:, width + top : width + 2 * top].astype(jnp.int32)
    pick, slot_share = route_tables(ids, counts, z_pos, tok_rows)

    def to_experts(rows):
        return lax.all_to_all(
            rows.reshape(X_SIZE, side, width),
            "exp",
            split_axis=0,
            concat_axis=0,
            tiled=True,
            axis_index_groups=X_GROUPS,
        )

    act_rows = jnp.dot(pick, act_all[:, :width], preferred_element_type=jnp.float32)
    input_rows = to_experts(act_rows.astype(jnp.bfloat16)).reshape(slot_count, width)
    cot_rows = jnp.dot(pick, cot_all, preferred_element_type=jnp.float32)
    cot_rows = (slot_share[:, None] * cot_rows).astype(jnp.bfloat16)
    cotan_rows = to_experts(cot_rows).reshape(slot_count, width)

    pre_acts = jnp.einsum(
        "sd,tdf->tsf", input_rows, whole_gate_up[0], preferred_element_type=jnp.float32
    )
    hidden_grad = jnp.einsum(
        "sd,fd->sf", cotan_rows, whole_down[0], preferred_element_type=jnp.float32
    )
    silu_val, silu_slope = silu_parts(pre_acts[0])
    gate_grad = (hidden_grad * pre_acts[1] * silu_slope).astype(jnp.bfloat16)
    up_grad = (hidden_grad * silu_val).astype(jnp.bfloat16)
    row_grad = (
        jnp.einsum("sf,df->sd", gate_grad, whole_gate_up[0, 0], preferred_element_type=jnp.float32)
        + jnp.einsum("sf,df->sd", up_grad, whole_gate_up[0, 1], preferred_element_type=jnp.float32)
    ).astype(jnp.bfloat16)
    home = to_experts(row_grad).reshape(slot_count, width)
    partial = jnp.einsum("st,sd->td", pick, home, preferred_element_type=jnp.float32)
    d_activation = lax.psum_scatter(
        partial.astype(jnp.bfloat16),
        "exp",
        scatter_dimension=0,
        tiled=True,
        axis_index_groups=Z_GROUPS,
    )

    hidden_width = gate_grad.shape[1]
    both_grads = jnp.concatenate([gate_grad, up_grad], axis=1)
    term = jnp.einsum("sd,sf->df", input_rows, both_grads, preferred_element_type=jnp.float32)
    term = lax.optimization_barrier(term.astype(jnp.bfloat16))
    local_square = jnp.sum(jnp.square(term.astype(jnp.float32)))
    summed = lax.psum_scatter(term, "rep", scatter_dimension=0, tiled=True).astype(jnp.float32)
    shard_rows = width // replicas
    grad_shard = summed.reshape(shard_rows, 2, hidden_width).transpose(1, 0, 2)
    small_sum, big_sum = lax.psum((local_square, jnp.sum(jnp.square(grad_shard))), "rep")
    entry_count = 2.0 * width * hidden_width
    small_norm = small_sum / (replicas * entry_count)
    big_norm = big_sum / (replicas * replicas * entry_count)
    noise_gain = replicas * big_norm / (small_norm + 1e-06)
    new_first = 0.9 * first_moment + 0.1 * grad_shard[None]
    new_second = 0.95 * second_moment + 0.05 * jnp.square(grad_shard[None])
    weight_step = (noise_gain * new_first / (jnp.sqrt(new_second) + 1e-08)).astype(jnp.bfloat16)
    return (d_activation, new_first, new_second, weight_step)


def solution(mesh):
    tokens = P(("rep", "exp"), None)
    shards = P("exp", None, "rep", None)
    return jax.shard_map(
        on_device,
        mesh=mesh,
        in_specs=(tokens,) * 5 + (shards, P("exp", None, "rep"), shards, shards),
        out_specs=(tokens, shards, shards, shards),
        check_vma=False,
    )
```
